32 devices in a mesh: groups: 2 (over y), sect: 16 (over z, x, core).
Axes of the slice: x: 2, y: 2, z: 4, core: 2. Of those that a mesh axis runs over, the one named last changes fastest.
Arguments:
- pattern: int32 [32], P('sect'), may hold values from 0 to 15
- thickness: float32 [32], P('sect'), may hold values from 0.5 to 1.5
- coupling: float32 [16, 2, 169, 169], replicated, may hold values from -0.0625 to 0.0625
- angles: float32 [64, 169], replicated, may hold values from -3.140625 to 3.140625
- points: int32 [2], P('groups'), parts along dimension 0, may hold values from 0 to 63
- incident: float32 [2, 2, 169, 169], P('groups'), parts along dimension 0, may hold values from -6 to 6
- monitors: int32 [16], replicated, may hold values from 0 to 168
- weights: float32 [16], replicated, may hold values from 0.05 to 0.5
Outputs:
- fields: float32 [32, 2, 2, 169, 169], P('sect', 'groups'), parts along dimension 1
- gradient: float32 [2, 32], P('groups', 'sect'), parts along dimension 0
The draws below stay inside these ranges and needn't reach their ends.
There are 2 independent parts, one for each index of `groups`. The reference program is written for one: setup_inputs(seed, part) draws one part's arguments, and reference() takes and returns one part's arrays. A program takes and returns all parts, laid end to end along the dimension named above; an argument that names none is the same for every part. Nothing has to cross between parts.
All inputs are finite; a program needn't handle non-finite values.
Results may differ from the reference program's by a relative error of at most 0.0003.
Values sent between devices are 32-bit elements; how exact they have to be, the bound alone decides.
A program may use at most 128 MiB of HBM per device.

```python
import math
import jax
import jax.numpy as jnp
from jax import lax

HARM = 169
NPAT = 16
NQ = 64
MON = 16
PTS = 1
LAYERS = 32


def place_ends(entries, key, smallest, top_value):
    longest = entries.shape.index(max(entries.shape))
    spots = []
    for shift in (0, 1):
        where = [jax.random.randint(jax.random.fold_in(key, axis), (), 0, length) for axis, length in enumerate(entries.shape)]
        where[longest] = (where[longest] + shift) % entries.shape[longest]
        spots.append(tuple(where))
    return entries.at[spots[0]].set(smallest).at[spots[1]].set(top_value)


def steps_of(own_key, shape, split, smallest, high):
    def one(dim, shards_of):
        heights = jax.random.uniform(jax.random.fold_in(jax.random.fold_in(own_key, 6), dim), (shards_of,), jnp.float32, smallest / len(split), high / len(split))
        return jnp.repeat(jnp.exp(heights), shape[dim] // shards_of).reshape((-1,) + (1,) * (len(shape) - dim - 1))

    factor_of = one(*split[0])
    for cut in split[1:]:
        factor_of = factor_of * one(*cut)
    return factor_of


def bell_draw(stream_key, dims, scale, limit, held_as=jnp.bfloat16):
    values = jax.random.normal(stream_key, dims, jnp.float32) * scale
    return jnp.minimum(jnp.maximum(values, -limit), limit).astype(held_as)


def setup_inputs(seed: int = 0, part: int = 0) -> dict:
    key_list = jax.random.split(jax.random.key(seed), 9)
    part_keys = jax.random.split(jax.random.fold_in(key_list[8], part), 9)
    pattern = place_ends(jax.random.randint(key_list[0], (LAYERS,), 0, NPAT), jax.random.fold_in(key_list[0], 1), 0, NPAT - 1).astype(jnp.int32)
    thickness = jnp.clip(jnp.exp(math.log(1.5) - 1.0986123 * jax.random.uniform(key_list[1], (LAYERS,), jnp.float32) ** steps_of(key_list[1], (LAYERS,), ((0, 16),), -0.2, 0.2)), 0.5, 1.5)
    coupling = bell_draw(key_list[2], (NPAT, 2, HARM, HARM), (44 * HARM) ** -0.5, 0.0625, jnp.float32)
    angles = jnp.clip(jax.random.uniform(key_list[3], (NQ, HARM), jnp.float32, -3.140625, 3.140625), -3.140625, 3.140625)
    points = jax.random.randint(part_keys[4], (PTS,), 0, NQ).astype(jnp.int32)
    incident = bell_draw(part_keys[5], (PTS, 2, HARM, HARM), 1.0, 6.0, jnp.float32)
    monitors = place_ends(jax.random.randint(key_list[6], (MON,), 0, HARM), jax.random.fold_in(key_list[6], 1), 0, HARM - 1).astype(jnp.int32)
    weights = jnp.clip(jnp.exp(jax.random.uniform(key_list[7], (MON,), jnp.float32, math.log(0.05), math.log(0.5))), 0.05, 0.5)
    return {"pattern": pattern, "thickness": thickness, "coupling": coupling, "angles": angles, "points": points, "incident": incident, "monitors": monitors, "weights": weights}


norm_scale = (1.0 + 1.0 / 22.0) ** -0.5
highest = lax.Precision.HIGHEST


def reference(pattern, thickness, coupling, angles, points, incident, monitors, weights):
    angle_rows = angles[points]
    point_count = incident.shape[0]
    identity_matrix = jnp.eye(HARM, dtype=jnp.float32)

    def forward(carried, inputs):
        pattern_id, layer_depth = inputs
        mixing_real = norm_scale * (identity_matrix + coupling[pattern_id, 0])
        mixing_imag = norm_scale * coupling[pattern_id, 1]
        field_real = carried[:, 0]
        field_imag = carried[:, 1]
        mixed_real = jnp.einsum("ij,pjk->pik", mixing_real, field_real, precision=highest) - jnp.einsum("ij,pjk->pik", mixing_imag, field_imag, precision=highest)
        mixed_imag = jnp.einsum("ij,pjk->pik", mixing_imag, field_real, precision=highest) + jnp.einsum("ij,pjk->pik", mixing_real, field_imag, precision=highest)
        cosine = jnp.cos(angle_rows * layer_depth)[:, :, None]
        sine_part = jnp.sin(angle_rows * layer_depth)[:, :, None]
        updated = jnp.stack([cosine * mixed_real - sine_part * mixed_imag, cosine * mixed_imag + sine_part * mixed_real], axis=1)
        return updated, updated

    last_field, fields = lax.scan(forward, incident, (pattern, thickness))
    selector = jnp.sum(jnp.where(monitors[:, None] == jnp.arange(HARM)[None, :], weights[:, None], 0.0), axis=0)
    adjoint = last_field * selector[None, None, :, None] / (point_count * HARM)

    def backward(carried, inputs):
        pattern_id, layer_depth, layer_field = inputs
        adj_real = carried[:, 0]
        adj_imag = carried[:, 1]
        contribution = -2.0 * jnp.sum(angle_rows[:, :, None] * (adj_real * layer_field[:, 1] - adj_imag * layer_field[:, 0]))
        cosine = jnp.cos(angle_rows * layer_depth)[:, :, None]
        sine_part = jnp.sin(angle_rows * layer_depth)[:, :, None]
        back_real = cosine * adj_real + sine_part * adj_imag
        back_imag = cosine * adj_imag - sine_part * adj_real
        mixing_real = norm_scale * (identity_matrix + coupling[pattern_id, 0])
        mixing_imag = norm_scale * coupling[pattern_id, 1]
        new_real = jnp.einsum("ji,pjk->pik", mixing_real, back_real, precision=highest) + jnp.einsum("ji,pjk->pik", mixing_imag, back_imag, precision=highest)
        new_imag = jnp.einsum("ji,pjk->pik", mixing_real, back_imag, precision=highest) - jnp.einsum("ji,pjk->pik", mixing_imag, back_real, precision=highest)
        return jnp.stack([new_real, new_imag], axis=1), contribution

    unused, gradient = lax.scan(backward, adjoint, (pattern, thickness, fields), reverse=True)
    return fields, gradient[None, :]
```

```python
import functools
import jax
import jax.numpy as jnp
from jax import lax
from jax.experimental import pallas as pl
from jax.experimental.pallas import tpu as pltpu
from jax.sharding import PartitionSpec as P

norm_scale = (1.0 + 1.0 / 22.0) ** (-0.5)
f32 = jnp.float32
bf16 = jnp.bfloat16


def gather_kernel(count, own_ref, out_ref, send_sem, recv_sem):
    here = lax.axis_index("sect")
    barrier = pltpu.get_barrier_semaphore()

    def peer(k):
        return lax.rem(here + k, count)

    def greet(k, c):
        pl.semaphore_signal(barrier, inc=1, device_id={"sect": peer(k)}, device_id_type=pl.DeviceIdType.MESH)
        return c

    lax.fori_loop(1, count, greet, 0)
    out_ref[here] = own_ref[...]
    pl.semaphore_wait(barrier, count - 1)

    def copy(k):
        return pltpu.make_async_remote_copy(
            src_ref=own_ref,
            dst_ref=out_ref.at[here],
            send_sem=send_sem.at[k],
            recv_sem=recv_sem.at[k],
            device_id={"sect": peer(k)},
            device_id_type=pl.DeviceIdType.MESH,
        )

    def start(k, c):
        copy(k).start()
        return c

    def finish(k, c):
        copy(k).wait()
        return c

    lax.fori_loop(1, count, start, 0)
    lax.fori_loop(1, count, finish, 0)


def split(x):
    hi = x.astype(bf16)
    return hi, (x - hi.astype(f32)).astype(bf16)


def dot(a, b, transposed):
    dims = (((1,), (1 if transposed else 0,)), ((), ()))
    return lax.dot_general(a, b, dims, preferred_element_type=f32)


def dot3(a, b, transposed):
    (ah, al), (bh, bl) = (a, b)
    return dot(ah, bh, transposed) + (dot(al, bh, transposed) + dot(ah, bl, transposed))


def main_kernel(
    sections, own_layers, gathered, points, monitors, weights, coupling, angles, incident,
    fields, gradient, parts, cosines, sines, kept,
):
    here = lax.axis_index("sect")
    layers = sections * own_layers
    patterns = coupling.shape[0]
    harm = incident.shape[-1]
    mon = monitors.shape[0]

    def pattern_of(layer):
        return gathered[layer // own_layers, 0, lax.rem(layer, own_layers)].astype(jnp.int32)

    def prepare(n, c):
        real, imag = coupling[n, 0], coupling[n, 1]
        for at, value in enumerate((real, imag, real + imag)):
            hi, lo = split(value)
            parts[n, 2 * at] = hi
            parts[n, 2 * at + 1] = lo
        return c

    lax.fori_loop(0, patterns, prepare, 0)

    theta = angles[pl.ds(points[0], 1), :]

    def fill(layer, c):
        depth = gathered[layer // own_layers, 0, own_layers + lax.rem(layer, own_layers)]
        cosines[pl.ds(layer, 1), :] = theta * depth
        return c

    lax.fori_loop(0, layers, fill, 0)
    phase = cosines[...]
    sines[...] = norm_scale * jnp.sin(phase)
    cosines[...] = norm_scale * jnp.cos(phase)

    rows = lax.broadcasted_iota(jnp.int32, (mon, harm), 0)
    lanes = lax.broadcasted_iota(jnp.int32, (mon, harm), 1)
    picked = jnp.zeros((mon, harm), f32)
    scale = jnp.zeros((mon, harm), f32)
    for m in range(mon):
        picked = jnp.where((rows == m) & (lanes == monitors[m]), 1.0, picked)
        scale = jnp.where(rows == m, weights[m], scale)
    scale = scale * (1.0 / harm)

    first = here * own_layers

    def forward(layer, real, imag):
        n = pattern_of(layer)
        one = dot3(split(real), (parts[n, 0], parts[n, 1]), True)
        two = dot3(split(imag), (parts[n, 2], parts[n, 3]), True)
        three = dot3(split(real + imag), (parts[n, 4], parts[n, 5]), True)
        mixed_real = real + (one - two)
        mixed_imag = imag + (three - one - two)
        cos, sin = cosines[pl.ds(layer, 1), :], sines[pl.ds(layer, 1), :]
        return cos * mixed_real - sin * mixed_imag, cos * mixed_imag + sin * mixed_real

    def backward(layer, both):
        @pl.when((layer >= first) & (layer < first + own_layers))
        def _():
            kept[layer - first] = both

        n = pattern_of(layer)
        real, imag = both[:mon], both[mon:]
        cos, sin = cosines[pl.ds(layer, 1), :], sines[pl.ds(layer, 1), :]
        both = jnp.concatenate([cos * real - sin * imag, cos * imag + sin * real], axis=0)
        hi, lo = split(both)
        stacked = jnp.concatenate([hi, lo], axis=0)

        def times(at):
            high = dot(stacked, parts[n, at], False)
            return high[: 2 * mon] + (high[2 * mon :] + dot(hi, parts[n, at + 1], False))

        by_real, by_imag = times(0), times(2)
        return both + jnp.concatenate(
            [by_real[:mon] - by_imag[mon:], by_real[mon:] + by_imag[:mon]], axis=0
        )

    def step(i, carry):
        real, imag, both = carry
        both = backward(layers - 1 - i, both)
        real, imag = forward(i, real, imag)
        return real, imag, both

    both = jnp.concatenate([picked, jnp.zeros_like(picked)], axis=0)
    carry = (incident[0, 0].T, incident[0, 1].T, both)
    real, imag, both = lax.fori_loop(0, first, step, carry)
    own = []
    for j in range(own_layers):
        real, imag, both = step(first + j, (real, imag, both))
        own.append((real, imag))
        fields[j, 0, 0] = real.T
        fields[j, 0, 1] = imag.T
    both = lax.fori_loop(
        first + own_layers, layers, lambda i, b: backward(layers - 1 - i, b), both
    )

    start = split(both)
    by_real = dot3(start, split(incident[0, 0]), False)
    by_imag = dot3(start, split(incident[0, 1]), False)
    out_real = scale * (by_real[:mon] - by_imag[mon:])
    out_imag = scale * (by_real[mon:] + by_imag[:mon])
    target = split(jnp.concatenate([out_real, out_imag], axis=0))
    for j in range(own_layers):
        real, imag = own[j]
        by_real = dot3(target, split(real), False)
        by_imag = dot3(target, split(imag), False)
        a_real = by_real[:mon] + by_imag[mon:]
        a_imag = by_imag[:mon] - by_real[mon:]
        now = kept[j]
        total = jnp.sum(theta * (now[:mon] * a_imag + now[mon:] * a_real))
        gradient[0, j] = -2.0 * total


def local(pattern, thickness, coupling, angles, points, incident, monitors, weights):
    sections = lax.axis_size("sect")
    own_layers = pattern.shape[0]
    harm = incident.shape[-1]
    layers = sections * own_layers
    vmem = pl.BlockSpec(memory_space=pltpu.VMEM)
    smem = pl.BlockSpec(memory_space=pltpu.SMEM)
    own = jnp.concatenate([pattern.astype(f32), thickness])
    own = jnp.pad(own, (0, 128 - own.shape[0]))[None]
    gathered = pl.pallas_call(
        functools.partial(gather_kernel, sections),
        out_shape=jax.ShapeDtypeStruct((sections, 1, 128), f32),
        in_specs=[vmem],
        out_specs=vmem,
        scratch_shapes=[pltpu.SemaphoreType.DMA((sections,)), pltpu.SemaphoreType.DMA((sections,))],
        compiler_params=pltpu.CompilerParams(collective_id=0, has_side_effects=True),
    )(own)
    return pl.pallas_call(
        functools.partial(main_kernel, sections, own_layers),
        out_shape=(
            jax.ShapeDtypeStruct((own_layers, 1, 2, harm, harm), f32),
            jax.ShapeDtypeStruct((1, own_layers), f32),
        ),
        in_specs=[smem, smem, smem, smem, vmem, vmem, vmem],
        out_specs=(vmem, smem),
        scratch_shapes=[
            pltpu.VMEM((coupling.shape[0], 6, harm, harm), bf16),
            pltpu.VMEM((layers, harm), f32),
            pltpu.VMEM((layers, harm), f32),
            pltpu.VMEM((own_layers, 2 * monitors.shape[0], harm), f32),
        ],
        compiler_params=pltpu.CompilerParams(vmem_limit_bytes=40 * 2**20),
    )(gathered, points, monitors, weights, coupling, angles, incident)


def solution(mesh):
    in_specs = (
        P("sect"), P("sect"), P(), P(), P("groups"),
        P("groups", None, None, None), P(), P(),
    )
    out_specs = (P("sect", "groups", None, None, None), P("groups", "sect"))
    return jax.shard_map(local, mesh=mesh, in_specs=in_specs, out_specs=out_specs, check_vma=False)
```

```python
import functools
import jax
import jax.numpy as jnp
from jax import lax
from jax.experimental import pallas as pl
from jax.experimental.pallas import tpu as pltpu
from jax.sharding import PartitionSpec as P

norm_scale = (1.0 + 1.0 / 22.0) ** (-0.5)
f32 = jnp.float32
bf16 = jnp.bfloat16


def split(x):
    hi = x.astype(bf16)
    return hi, (x - hi.astype(f32)).astype(bf16)


def dot(a, b, transposed):
    dims = (((1,), (1 if transposed else 0,)), ((), ()))
    return lax.dot_general(a, b, dims, preferred_element_type=f32)


def dot3(a, b, transposed):
    (ah, al), (bh, bl) = (a, b)
    return dot(ah, bh, transposed) + (dot(al, bh, transposed) + dot(ah, bl, transposed))


MESH = pl.DeviceIdType.MESH
cores = 2


def main_kernel(
    sections, own_layers, pattern, thickness, points, monitors, weights, coupling, angles, incident,
    fields, gradient, table, parts, start_fields, cosines, sines, kept, angle_rows, inc, whole, leaving,
    ids, depths, ids_smem, depths_smem,
    load_sem, more_sem, small_sem, send_sem, recv_sem, swap_send, swap_recv,
):
    here = lax.axis_index("sect")
    layers = sections * own_layers
    patterns = coupling.shape[0]
    harm = incident.shape[-1]
    mon = monitors.shape[0]
    share = leaving.shape[2]
    core = lax.rem(here, cores)
    chip_first = (here - core) * own_layers
    first = here * own_layers
    barrier = pltpu.get_barrier_semaphore()

    def peer(k):
        return lax.rem(here + k, sections)

    def greet(k, c):
        pl.semaphore_signal(barrier, inc=1, device_id={"sect": peer(k)}, device_id_type=MESH)
        return c

    lax.fori_loop(1, sections, greet, 0)

    def load(n):
        return pltpu.make_async_copy(coupling.at[n], table.at[n], load_sem.at[n])

    def load_start(n, c):
        load(n).start()
        return c

    more = (
        pltpu.make_async_copy(incident, inc, more_sem.at[0]),
        pltpu.make_async_copy(angles, angle_rows, more_sem.at[1]),
    )
    lax.fori_loop(0, patterns, load_start, 0)
    for copy in more:
        copy.start()

    lane = lax.broadcasted_iota(jnp.int32, (1, 128), 1)
    id_row = jnp.zeros((1, 128), jnp.int32)
    depth_row = jnp.zeros((1, 128), f32)
    for j in range(own_layers):
        id_row = jnp.where(lane == j, pattern[j], id_row)
        depth_row = jnp.where(lane == j, thickness[j], depth_row)
    ids[here] = id_row
    depths[here] = depth_row
    pl.semaphore_wait(barrier, sections - 1)

    def sends(k):
        return tuple(
            pltpu.make_async_remote_copy(
                src_ref=rows.at[here],
                dst_ref=rows.at[here],
                send_sem=send_sem.at[at, k],
                recv_sem=recv_sem.at[at, k],
                device_id={"sect": peer(k)},
                device_id_type=MESH,
            )
            for at, rows in enumerate((ids, depths))
        )

    def send_start(k, c):
        for copy in sends(k):
            copy.start()
        return c

    def send_finish(k, c):
        for copy in sends(k):
            copy.wait()
        return c

    lax.fori_loop(1, sections, send_start, 0)

    def prepare(n, c):
        load(n).wait()
        real, imag = table[n, :, 0, :], table[n, :, 1, :]
        for at, value in enumerate((real, imag, real + imag)):
            hi, lo = split(value)
            parts[n, 2 * at] = hi
            parts[n, 2 * at + 1] = lo
        return c

    lax.fori_loop(0, patterns, prepare, 0)
    for copy in more:
        copy.wait()
    for c in range(2):
        start_fields[c] = jnp.zeros_like(start_fields[c])
        start_fields[c, :harm, :] = inc[0, :, c, :].T
    theta = angle_rows[pl.ds(points[0], 1), :]

    rows = lax.broadcasted_iota(jnp.int32, (mon, harm), 0)
    lanes = lax.broadcasted_iota(jnp.int32, (mon, harm), 1)
    picked = jnp.zeros((mon, harm), f32)
    scale = jnp.zeros((mon, harm), f32)
    for m in range(mon):
        picked = jnp.where((rows == m) & (lanes == monitors[m]), 1.0, picked)
        scale = jnp.where(rows == m, weights[m], scale)
    scale = scale * (1.0 / harm)

    lax.fori_loop(1, sections, send_finish, 0)
    small = (
        pltpu.make_async_copy(ids, ids_smem, small_sem.at[0]),
        pltpu.make_async_copy(depths, depths_smem, small_sem.at[1]),
    )
    for copy in small:
        copy.start()
    for copy in small:
        copy.wait()

    def pattern_of(layer):
        return ids_smem[layer // own_layers, 0, lax.rem(layer, own_layers)]

    def fill(layer, c):
        depth = depths_smem[layer // own_layers, 0, lax.rem(layer, own_layers)]
        cosines[pl.ds(layer, 1), :] = theta * depth
        return c

    lax.fori_loop(0, layers, fill, 0)
    phase = cosines[...]
    sines[...] = norm_scale * jnp.sin(phase)
    cosines[...] = norm_scale * jnp.cos(phase)

    def forward(layer, real, imag):
        n = pattern_of(layer)
        one = dot3(split(real), (parts[n, 0], parts[n, 1]), True)
        two = dot3(split(imag), (parts[n, 2], parts[n, 3]), True)
        three = dot3(split(real + imag), (parts[n, 4], parts[n, 5]), True)
        mixed_real = real + (one - two)
        mixed_imag = imag + (three - one - two)
        cos, sin = cosines[pl.ds(layer, 1), :], sines[pl.ds(layer, 1), :]
        return cos * mixed_real - sin * mixed_imag, cos * mixed_imag + sin * mixed_real

    def backward(layer, both):
        @pl.when((layer >= first) & (layer < first + own_layers))
        def _():
            kept[layer - first] = both

        n = pattern_of(layer)
        real, imag = both[:mon], both[mon:]
        cos, sin = cosines[pl.ds(layer, 1), :], sines[pl.ds(layer, 1), :]
        both = jnp.concatenate([cos * real - sin * imag, cos * imag + sin * real], axis=0)
        hi, lo = split(both)
        stacked = jnp.concatenate([hi, lo], axis=0)

        def times(at):
            high = dot(stacked, parts[n, at], False)
            return high[: 2 * mon] + (high[2 * mon :] + dot(hi, parts[n, at + 1], False))

        by_real, by_imag = times(0), times(2)
        return both + jnp.concatenate(
            [by_real[:mon] - by_imag[mon:], by_real[mon:] + by_imag[:mon]], axis=0
        )

    def step(i, carry):
        real, imag, both = carry
        both = backward(layers - 1 - i, both)
        real, imag = forward(i, real, imag)
        return real, imag, both

    own_rows = pl.ds(pl.multiple_of(core * share, 8), share)

    def swap(j):
        return pltpu.make_async_remote_copy(
            src_ref=leaving.at[j],
            dst_ref=whole.at[j, :, own_rows, :],
            send_sem=swap_send.at[j],
            recv_sem=swap_recv.at[j],
            device_id={"sect": here + 1 - 2 * core},
            device_id_type=MESH,
        )

    both = jnp.concatenate([picked, jnp.zeros_like(picked)], axis=0)
    carry = (start_fields[0, own_rows, :], start_fields[1, own_rows, :], both)
    real, imag, both = lax.fori_loop(0, chip_first, step, carry)
    for owner in range(cores):
        for j in range(own_layers):
            i = chip_first + owner * own_layers + j
            real, imag, both = step(i, (real, imag, both))

            @pl.when(core == owner)
            def _():
                whole[j, 0, own_rows, :] = real
                whole[j, 1, own_rows, :] = imag

            @pl.when(core != owner)
            def _():
                leaving[j, 0] = real
                leaving[j, 1] = imag
                swap(j).start()

    both = lax.fori_loop(
        chip_first + cores * own_layers, layers, lambda i, b: backward(layers - 1 - i, b), both
    )

    start = split(both)
    by_real = dot3(start, split(inc[0, :, 0, :]), False)
    by_imag = dot3(start, split(inc[0, :, 1, :]), False)
    out_real = scale * (by_real[:mon] - by_imag[mon:])
    out_imag = scale * (by_real[mon:] + by_imag[:mon])
    target = split(jnp.concatenate([out_real, out_imag], axis=0))
    for j in range(own_layers):
        swap(j).wait()
        real, imag = whole[j, 0, :harm, :], whole[j, 1, :harm, :]
        fields[j, 0, :, 0, :] = real.T
        fields[j, 0, :, 1, :] = imag.T
        by_real = dot3(target, split(real), False)
        by_imag = dot3(target, split(imag), False)
        a_real = by_real[:mon] + by_imag[mon:]
        a_imag = by_imag[:mon] - by_real[mon:]
        now = kept[j]
        total = jnp.sum(theta * (now[:mon] * a_imag + now[mon:] * a_real))
        gradient[0, j] = -2.0 * total


def local(pattern, thickness, coupling, angles, points, incident, monitors, weights):
    sections = lax.axis_size("sect")
    own_layers = pattern.shape[0]
    patterns = coupling.shape[0]
    harm = incident.shape[-1]
    layers = sections * own_layers
    share = -(-harm // (8 * cores)) * 8
    vmem = pl.BlockSpec(memory_space=pltpu.VMEM)
    smem = pl.BlockSpec(memory_space=pltpu.SMEM)
    hbm = pl.BlockSpec(memory_space=pltpu.HBM)
    dma = pltpu.SemaphoreType.DMA
    fields, gradient = pl.pallas_call(
        functools.partial(main_kernel, sections, own_layers),
        out_shape=(
            jax.ShapeDtypeStruct((own_layers, 1, harm, 2, harm), f32),
            jax.ShapeDtypeStruct((1, own_layers), f32),
        ),
        in_specs=[smem] * 5 + [hbm] * 3,
        out_specs=(vmem, smem),
        scratch_shapes=[
            pltpu.VMEM((patterns, harm, 2, harm), f32),
            pltpu.VMEM((patterns, 6, harm, harm), bf16),
            pltpu.VMEM((2, cores * share, harm), f32),
            pltpu.VMEM((layers, harm), f32),
            pltpu.VMEM((layers, harm), f32),
            pltpu.VMEM((own_layers, 2 * monitors.shape[0], harm), f32),
            pltpu.VMEM(angles.shape, f32),
            pltpu.VMEM((1, harm, 2, harm), f32),
            pltpu.VMEM((own_layers, 2, cores * share, harm), f32),
            pltpu.VMEM((own_layers, 2, share, harm), f32),
            pltpu.VMEM((sections, 1, 128), jnp.int32),
            pltpu.VMEM((sections, 1, 128), f32),
            pltpu.SMEM((sections, 1, 128), jnp.int32),
            pltpu.SMEM((sections, 1, 128), f32),
            dma((patterns,)),
            dma((2,)),
            dma((2,)),
            dma((2, sections)),
            dma((2, sections)),
            dma((own_layers,)),
            dma((own_layers,)),
        ],
        compiler_params=pltpu.CompilerParams(
            collective_id=0, has_side_effects=True, vmem_limit_bytes=63 * 2**20
        ),
    )(
        pattern, thickness, points, monitors, weights,
        coupling.transpose(0, 2, 1, 3), angles, incident.transpose(0, 2, 1, 3),
    )
    return fields.transpose(0, 1, 3, 2, 4), gradient


def solution(mesh):
    in_specs = (
        P("sect"), P("sect"), P(), P(), P("groups"),
        P("groups", None, None, None), P(), P(),
    )
    out_specs = (P("sect", "groups", None, None, None), P("groups", "sect"))
    return jax.shard_map(local, mesh=mesh, in_specs=in_specs, out_specs=out_specs, check_vma=False)
```

```python
import functools
import jax
import jax.numpy as jnp
from jax import lax
from jax.experimental import pallas as pl
from jax.experimental.pallas import tpu as pltpu
from jax.sharding import PartitionSpec as P

norm_scale = (1.0 + 1.0 / 22.0) ** (-0.5)
f32 = jnp.float32
bf16 = jnp.bfloat16


def gather_kernel(count, own_ref, out_ref, send_sem, recv_sem):
    here = lax.axis_index("sect")
    barrier = pltpu.get_barrier_semaphore()

    def peer(k):
        return lax.rem(here + k, count)

    def greet(k, c):
        pl.semaphore_signal(barrier, inc=1, device_id={"sect": peer(k)}, device_id_type=pl.DeviceIdType.MESH)
        return c

    lax.fori_loop(1, count, greet, 0)
    out_ref[here] = own_ref[...]
    pl.semaphore_wait(barrier, count - 1)

    def copy(k):
        return pltpu.make_async_remote_copy(
            src_ref=own_ref,
            dst_ref=out_ref.at[here],
            send_sem=send_sem.at[k],
            recv_sem=recv_sem.at[k],
            device_id={"sect": peer(k)},
            device_id_type=pl.DeviceIdType.MESH,
        )

    def start(k, c):
        copy(k).start()
        return c

    def finish(k, c):
        copy(k).wait()
        return c

    lax.fori_loop(1, count, start, 0)
    lax.fori_loop(1, count, finish, 0)


def split(x):
    hi = x.astype(bf16)
    return hi, (x - hi.astype(f32)).astype(bf16)


def dot(a, b, transposed):
    dims = (((1,), (1 if transposed else 0,)), ((), ()))
    return lax.dot_general(a, b, dims, preferred_element_type=f32)


def dot3(a, b, transposed):
    (ah, al), (bh, bl) = (a, b)
    return dot(ah, bh, transposed) + (dot(al, bh, transposed) + dot(ah, bl, transposed))


def main_kernel(
    sections, own_layers, gathered, points, monitors, weights, coupling, angles, incident,
    fields, gradient, parts, cosines, sines, kept,
):
    here = lax.axis_index("sect")
    layers = sections * own_layers
    patterns = coupling.shape[0]
    harm = incident.shape[-1]
    mon = monitors.shape[0]

    def pattern_of(layer):
        return gathered[layer // own_layers, 0, lax.rem(layer, own_layers)].astype(jnp.int32)

    def prepare(n, c):
        real, imag = coupling[n, :, 0, :], coupling[n, :, 1, :]
        for at, value in enumerate((real, imag, real + imag)):
            hi, lo = split(value)
            parts[n, 2 * at] = hi
            parts[n, 2 * at + 1] = lo
        return c

    lax.fori_loop(0, patterns, prepare, 0)

    theta = angles[pl.ds(points[0], 1), :]

    def fill(layer, c):
        depth = gathered[layer // own_layers, 0, own_layers + lax.rem(layer, own_layers)]
        cosines[pl.ds(layer, 1), :] = theta * depth
        return c

    lax.fori_loop(0, layers, fill, 0)
    phase = cosines[...]
    sines[...] = norm_scale * jnp.sin(phase)
    cosines[...] = norm_scale * jnp.cos(phase)

    rows = lax.broadcasted_iota(jnp.int32, (mon, harm), 0)
    lanes = lax.broadcasted_iota(jnp.int32, (mon, harm), 1)
    picked = jnp.zeros((mon, harm), f32)
    scale = jnp.zeros((mon, harm), f32)
    for m in range(mon):
        picked = jnp.where((rows == m) & (lanes == monitors[m]), 1.0, picked)
        scale = jnp.where(rows == m, weights[m], scale)
    scale = scale * (1.0 / harm)

    first = here * own_layers

    def forward(layer, real, imag):
        n = pattern_of(layer)
        one = dot3(split(real), (parts[n, 0], parts[n, 1]), True)
        two = dot3(split(imag), (parts[n, 2], parts[n, 3]), True)
        three = dot3(split(real + imag), (parts[n, 4], parts[n, 5]), True)
        mixed_real = real + (one - two)
        mixed_imag = imag + (three - one - two)
        cos, sin = cosines[pl.ds(layer, 1), :], sines[pl.ds(layer, 1), :]
        return cos * mixed_real - sin * mixed_imag, cos * mixed_imag + sin * mixed_real

    def backward(layer, both):
        @pl.when((layer >= first) & (layer < first + own_layers))
        def _():
            kept[layer - first] = both

        n = pattern_of(layer)
        real, imag = both[:mon], both[mon:]
        cos, sin = cosines[pl.ds(layer, 1), :], sines[pl.ds(layer, 1), :]
        both = jnp.concatenate([cos * real - sin * imag, cos * imag + sin * real], axis=0)
        hi, lo = split(both)
        stacked = jnp.concatenate([hi, lo], axis=0)

        def times(at):
            high = dot(stacked, parts[n, at], False)
            return high[: 2 * mon] + (high[2 * mon :] + dot(hi, parts[n, at + 1], False))

        by_real, by_imag = times(0), times(2)
        return both + jnp.concatenate(
            [by_real[:mon] - by_imag[mon:], by_real[mon:] + by_imag[:mon]], axis=0
        )

    def step(i, carry):
        real, imag, both = carry
        both = backward(layers - 1 - i, both)
        real, imag = forward(i, real, imag)
        return real, imag, both

    both = jnp.concatenate([picked, jnp.zeros_like(picked)], axis=0)
    carry = (incident[0, :, 0, :].T, incident[0, :, 1, :].T, both)
    real, imag, both = lax.fori_loop(0, first, step, carry)
    own = []
    for j in range(own_layers):
        real, imag, both = step(first + j, (real, imag, both))
        own.append((real, imag))
        fields[j, 0, :, 0, :] = real.T
        fields[j, 0, :, 1, :] = imag.T
    both = lax.fori_loop(
        first + own_layers, layers, lambda i, b: backward(layers - 1 - i, b), both
    )

    start = split(both)
    by_real = dot3(start, split(incident[0, :, 0, :]), False)
    by_imag = dot3(start, split(incident[0, :, 1, :]), False)
    out_real = scale * (by_real[:mon] - by_imag[mon:])
    out_imag = scale * (by_real[mon:] + by_imag[:mon])
    target = split(jnp.concatenate([out_real, out_imag], axis=0))
    for j in range(own_layers):
        real, imag = own[j]
        by_real = dot3(target, split(real), False)
        by_imag = dot3(target, split(imag), False)
        a_real = by_real[:mon] + by_imag[mon:]
        a_imag = by_imag[:mon] - by_real[mon:]
        now = kept[j]
        total = jnp.sum(theta * (now[:mon] * a_imag + now[mon:] * a_real))
        gradient[0, j] = -2.0 * total


def local(pattern, thickness, coupling, angles, points, incident, monitors, weights):
    sections = lax.axis_size("sect")
    own_layers = pattern.shape[0]
    harm = incident.shape[-1]
    layers = sections * own_layers
    vmem = pl.BlockSpec(memory_space=pltpu.VMEM)
    smem = pl.BlockSpec(memory_space=pltpu.SMEM)
    own = jnp.concatenate([pattern.astype(f32), thickness])
    own = jnp.pad(own, (0, 128 - own.shape[0]))[None]
    gathered = pl.pallas_call(
        functools.partial(gather_kernel, sections),
        out_shape=jax.ShapeDtypeStruct((sections, 1, 128), f32),
        in_specs=[vmem],
        out_specs=vmem,
        scratch_shapes=[pltpu.SemaphoreType.DMA((sections,)), pltpu.SemaphoreType.DMA((sections,))],
        compiler_params=pltpu.CompilerParams(collective_id=0, has_side_effects=True),
    )(own)
    fields, gradient = pl.pallas_call(
        functools.partial(main_kernel, sections, own_layers),
        out_shape=(
            jax.ShapeDtypeStruct((own_layers, 1, harm, 2, harm), f32),
            jax.ShapeDtypeStruct((1, own_layers), f32),
        ),
        in_specs=[smem, smem, smem, smem, vmem, vmem, vmem],
        out_specs=(vmem, smem),
        scratch_shapes=[
            pltpu.VMEM((coupling.shape[0], 6, harm, harm), bf16),
            pltpu.VMEM((layers, harm), f32),
            pltpu.VMEM((layers, harm), f32),
            pltpu.VMEM((own_layers, 2 * monitors.shape[0], harm), f32),
        ],
        compiler_params=pltpu.CompilerParams(vmem_limit_bytes=40 * 2**20),
    )(
        gathered, points, monitors, weights,
        coupling.transpose(0, 2, 1, 3), angles, incident.transpose(0, 2, 1, 3),
    )
    return fields.transpose(0, 1, 3, 2, 4), gradient


def solution(mesh):
    in_specs = (
        P("sect"), P("sect"), P(), P(), P("groups"),
        P("groups", None, None, None), P(), P(),
    )
    out_specs = (P("sect", "groups", None, None, None), P("groups", "sect"))
    return jax.shard_map(local, mesh=mesh, in_specs=in_specs, out_specs=out_specs, check_vma=False)
```
